256 devices in a mesh: cuts: 8 (over z), dev: 32 (over x, y, core).
Axes of the slice: x: 4, y: 4, z: 8, core: 2. Of those that a mesh axis runs over, the one named last changes fastest.
Arguments:
- inputs: bfloat16 [131072, 3072], P(('cuts', 'dev')), may hold values from -6 to 6
- cotangent: bfloat16 [131072, 512], P(('cuts', 'dev')), may hold values from -0.29882812 to 0.29882812
- errors: bfloat16 [256, 3072, 512], P(('cuts', 'dev')), may hold values from -6 to 6
- previous_q: float32 [512, 64], replicated, may hold values from -0.25 to 0.25
Outputs:
- new_errors: bfloat16 [256, 3072, 512], P(('cuts', 'dev'))
- p_hat: float32 [3072, 64], replicated
- q_mean: float32 [512, 64], replicated
The draws below stay inside these ranges and needn't reach their ends.
All inputs are finite; a program needn't handle non-finite values.
Results may differ from the reference program's by a relative error of at most 0.001.
Values sent between devices are 32-bit elements; how exact they have to be, the bound alone decides.
A program may use at most 64 MiB of HBM per device.

```python
import jax
import jax.numpy as jnp
from jax import lax

D = 3072
KVW = 512
RANK = 64
TOK_DEV = 512
TOKENS = 131072
N_CUTS = 8
N_DEV = 32
DEVICES = 256


def block_scale(key, extent, cuts, low, high):
    def one(axis_at, shards_of):
        steps = jax.random.uniform(jax.random.fold_in(jax.random.fold_in(key, 6), axis_at), (shards_of,), jnp.float32, low / len(cuts), high / len(cuts))
        return jnp.repeat(jnp.exp(steps), extent[axis_at] // shards_of).reshape((-1,) + (1,) * (len(extent) - axis_at - 1))

    loudness = one(*cuts[0])
    for cut in cuts[1:]:
        loudness = loudness * one(*cut)
    return loudness


def gaussian(rng, dims, width, bound, cuts=(), held_as=jnp.bfloat16):
    drawn = jax.random.normal(rng, dims, jnp.float32) * width
    if len(cuts) > 0:
        drawn = block_scale(rng, dims, cuts, -0.22, 0.18) * drawn
    return jnp.clip(drawn, min=-bound, max=bound).astype(held_as)


def setup_inputs(seed: int = 0) -> dict:
    key_of = jax.random.split(jax.random.key(seed), 5)
    return {
        "inputs": gaussian(key_of[0], (TOKENS, D), 1.0, 6.0, ((0, 256),)),
        "cotangent": gaussian(key_of[1], (TOKENS, KVW), 0.05, 0.29882812, ((0, 256),)),
        "errors": gaussian(key_of[2], (DEVICES, D, KVW), 1.0, 6.0, ((0, 256),)),
        "previous_q": gaussian(key_of[3], (KVW, RANK), KVW ** -0.5, 0.25, (), jnp.float32),
    }


HI = lax.Precision.HIGHEST

def orthonormal(p_sum):
    gram = jnp.dot(p_sum.T, p_sum, precision=HI)
    lower = jnp.linalg.cholesky(gram)
    return lax.linalg.triangular_solve(lower, p_sum, left_side=False, lower=True, transpose_a=True)

def reference(inputs, cotangent, errors, previous_q):
    count = N_CUTS * N_DEV
    xs = inputs.reshape(count, TOK_DEV, D)
    ys = cotangent.reshape(count, TOK_DEV, KVW)

    def p_step(acc, triple):
        xw, yw, ew = triple
        xf = xw.astype(jnp.float32)
        yf = yw.astype(jnp.float32)
        term = jnp.dot(xf.T, jnp.dot(yf, previous_q, precision=HI), precision=HI)
        term = term + jnp.dot(ew.astype(jnp.float32), previous_q, precision=HI)
        return (acc + term, None)
    p_sum, _ = lax.scan(p_step, jnp.zeros((D, RANK), jnp.float32), (xs, ys, errors))
    p_hat = orthonormal(p_sum)

    def q_step(acc, triple):
        xw, yw, ew = triple
        xf = xw.astype(jnp.float32)
        yf = yw.astype(jnp.float32)
        term = jnp.dot(yf.T, jnp.dot(xf, p_hat, precision=HI), precision=HI)
        term = term + jnp.dot(ew.astype(jnp.float32).T, p_hat, precision=HI)
        return (acc + term, None)
    q_sum, _ = lax.scan(q_step, jnp.zeros((KVW, RANK), jnp.float32), (xs, ys, errors))
    q_mean = q_sum / count
    approx = jnp.dot(p_hat, q_mean.T, precision=HI)

    def refresh(triple):
        xw, yw, ew = triple
        merged = jnp.dot(xw.astype(jnp.float32).T, yw.astype(jnp.float32), precision=HI) + ew.astype(jnp.float32)
        return (merged - approx).astype(jnp.bfloat16)
    new_errors = lax.map(refresh, (xs, ys, errors))
    return (new_errors, p_hat, q_mean)
```

```python
import functools

import jax
import jax.numpy as jnp
from jax import lax
from jax.experimental import pallas as pl
from jax.experimental.pallas import tpu as pltpu
from jax.sharding import PartitionSpec as P

MESH = pl.DeviceIdType.MESH
F32 = jnp.float32
BF16 = jnp.bfloat16
SUBS = 3


def halves(value):
    high = value.astype(BF16)
    low = (value - high.astype(F32)).astype(BF16)
    return high, low


def mm(left, right, left_dim=1, right_dim=0):
    return lax.dot_general(
        left, right, (((left_dim,), (right_dim,)), ((), ())), preferred_element_type=F32
    )


def kernel(
    nx, ny, nz,
    x_hbm, y_hbm, e_hbm, qt_ref,
    out_ref, phat_ref, qmean_ref,
    xv, ev, yv, merged, m_high, m_low, base,
    part, core_in, chip_sum, plane_in, z_in, full,
    g_own, g_in, gz_in, g_tile, g_full, aug,
    load_sem, core_send, core_recv, rs_send, rs_recv, z_send, z_recv,
    ag_send, ag_recv, fw_send, fw_recv, g_sem,
):
    subs = SUBS
    rank, kvw = qt_ref.shape
    pieces, tok, width = xv.shape
    group = rank // (2 * ny)
    devices = nx * ny * 2 * nz
    z = lax.axis_index("cuts")
    d = lax.axis_index("dev")
    x, y, c = d // (2 * ny), (d // 2) % ny, d % 2

    def at(xx, yy, cc):
        return (z, (xx * ny + yy) * 2 + cc)

    def away(value, step, n):
        return lax.rem(value + step, n)

    partner = at(x, y, 1 - c)

    def remote(src, dst, send, recv, device):
        return pltpu.make_async_remote_copy(
            src_ref=src, dst_ref=dst, send_sem=send, recv_sem=recv, device_id=device, device_id_type=MESH
        )

    def wait_bytes(ref, sem):
        pltpu.make_async_copy(ref, ref, sem).wait()

    x_steps = [(s + nx // 2) % nx for s in range(nx)]
    order = [(s, step) for s in range(subs) for step in [t for t in x_steps if t] + [0]]

    def place(s, step):
        return away(x, step, nx) * subs + s

    y_load = pltpu.make_async_copy(y_hbm, yv, load_sem.at[2, 0])
    y_load.start()
    loads = []
    for i, (s, step) in enumerate(order):
        a = place(s, step)
        start = pl.multiple_of(a * width, width)
        loads.append((
            pltpu.make_async_copy(e_hbm.at[0, pl.ds(start, width), :], ev.at[i], load_sem.at[1, i]),
            pltpu.make_async_copy(x_hbm.at[:, pl.ds(start, width)], xv.at[i], load_sem.at[0, i]),
        ))
        loads[-1][0].start()
        loads[-1][1].start()

    barrier = pltpu.get_barrier_semaphore()
    for k in range(1, 2 * nx * ny):
        pl.semaphore_signal(barrier, inc=1, device_id=(z, away(d, k, 2 * nx * ny)), device_id_type=MESH)
    for k in range(1, nz):
        pl.semaphore_signal(barrier, inc=1, device_id=(away(z, k, nz), d), device_id_type=MESH)

    q_high, q_low = halves(qt_ref[...])
    q_two = jnp.concatenate([q_high, q_low], axis=0)
    y_load.wait()
    t_two = mm(q_two, yv[...], 1, 1)
    t_high, t_low = halves(t_two[:rank] + t_two[rank:])
    base[0:rank, :] = t_high
    base[rank:2 * rank, :] = t_low
    base[2 * rank:4 * rank, :] = q_two

    def left_piece(i):
        for load in loads[i]:
            load.wait()
        both = mm(base[0:2 * rank, :], xv[i]) + mm(base[2 * rank:4 * rank, :], ev[i], 1, 1)
        value = both[:rank] + both[rank:]
        part[i] = value.reshape(2 * ny, group, width)

    def core_copy(i):
        return remote(
            part.at[i, pl.ds((1 - c) * ny, ny)], core_in.at[i], core_send.at[i], core_recv.at[i], partner
        )

    def scatter(i):
        s, step = order[i]
        core_copy(i).wait_recv()
        chip_sum[i] = part[i, pl.ds(c * ny, ny)] + core_in[i]
        for dy in range(ny):
            if step == 0 and dy == 0:
                continue
            slot = ((nx - step) % nx) * ny + (ny - dy) % ny - 1
            yy = away(y, dy, ny)
            remote(
                chip_sum.at[i, yy], plane_in.at[s, slot], rs_send, rs_recv.at[s], at(away(x, step, nx), yy, c)
            ).start()

    def merge_piece(i):
        s, step = order[i]
        a = place(s, step)
        value = mm(xv[i], yv[...], 0, 0) + ev[i].astype(F32)
        merged[a] = value
        high, low = halves(value)
        m_high[a] = high
        m_low[a] = low

    lag = 2
    for i in range(pieces):
        left_piece(i)
        if i == 0:
            pl.semaphore_wait(barrier, 2 * nx * ny - 1 + nz - 1)
        core_copy(i).start()
        if i >= lag:
            scatter(i - lag)
    for i in range(pieces - lag, pieces):
        scatter(i)

    own = [i for i in range(pieces) if order[i][1] == 0]

    def exchange(s):
        wait_bytes(plane_in.at[s], rs_recv.at[s])
        total = chip_sum[own[s], y]
        for slot in range(nx * ny - 1):
            total = total + plane_in[s, slot]
        z_in[s, z] = total
        for k in range(1, nz):
            remote(z_in.at[s, z], z_in.at[s, z], z_send, z_recv.at[s], (away(z, k, nz), d)).start()

    row = c * ny + y

    def spread(s):
        wait_bytes(z_in.at[s, pl.ds(0, nz - 1)], z_recv.at[s])
        total = z_in[s, 0]
        for k in range(1, nz):
            total = total + z_in[s, k]
        a = place(s, 0)
        full[a, row] = total
        for dx in [t for t in x_steps if t] + [0]:
            for dy in range(ny):
                if dx == 0 and dy == 0:
                    continue
                remote(
                    full.at[a, row], full.at[a, row], ag_send, ag_recv.at[s, (nx - dx) % nx],
                    at(away(x, dx, nx), away(y, dy, ny), c),
                ).start()

    half = pieces // 2
    for i in range(half):
        merge_piece(i)
    rest = list(range(half, pieces))
    for s in range(subs):
        exchange(s)
        for i in rest[s * (pieces - half) // subs:(s + 1) * (pieces - half) // subs]:
            merge_piece(i)
    for s in range(subs):
        spread(s)

    near = [0] + [t for t in range(1, nx) if t in (1, nx - 1)] + [t for t in range(2, nx - 1)]
    arrivals = [(s, rx) for s in range(subs) for rx in near]

    def forward(s, rx):
        a = place(s, rx)
        count = ny - 1 if rx == 0 else ny
        wait_bytes(full.at[a, pl.ds(c * ny, count)], ag_recv.at[s, rx])
        mine = full.at[a, pl.ds(c * ny, ny)]
        remote(mine, mine, fw_send, fw_recv.at[s, rx], partner).start()

    def right_piece(s, rx, first):
        a = place(s, rx)
        theirs = full.at[a, pl.ds((1 - c) * ny, ny)]
        wait_bytes(theirs, fw_recv.at[s, rx])
        high, low = halves(full[a].reshape(rank, width))
        two = mm(jnp.concatenate([high, low], axis=0), m_high[a])
        value = two[:rank] + two[rank:] + mm(high, m_low[a])
        if first:
            g_own[...] = value
        else:
            g_own[...] += value

    for i, (s, rx) in enumerate(arrivals):
        forward(s, rx)
        if i >= 1:
            right_piece(*arrivals[i - 1], i == 1)
    right_piece(*arrivals[-1], False)

    g_cols = kvw // nx

    def tile(ref, xx, rr):
        return ref.at[pl.ds(pl.multiple_of(rr * group, group), group), pl.ds(pl.multiple_of(xx * g_cols, g_cols), g_cols)]

    n_dev = 2 * nx * ny
    for k in range(1, n_dev):
        to = away(d, k, n_dev)
        tx, ty, tc = to // (2 * ny), (to // 2) % ny, to % 2
        remote(tile(g_own, tx, tc * ny + ty), g_in.at[n_dev - k - 1], g_sem.at[0], g_sem.at[1], (z, to)).start()

    gram = jnp.zeros((2 * rank, 2 * rank), F32)
    for a in range(pieces):
        high, low = halves(full[a].reshape(rank, width))
        two = jnp.concatenate([high, low], axis=0)
        gram = gram + mm(two, two, 1, 1)
    gram = gram[:rank] + gram[rank:]
    gram = gram[:, :rank] + gram[:, rank:]
    rows = lax.broadcasted_iota(jnp.int32, (rank, 2 * rank), 0)
    lanes = lax.broadcasted_iota(jnp.int32, (rank, 2 * rank), 1)
    aug[:, 0:rank] = gram
    aug[:, rank:2 * rank] = (rows == lanes).astype(F32)[:, :rank]

    def eliminate(k, carry):
        value = aug[...]
        pivot_row = aug[pl.ds(k, 1), :]
        column = jnp.sum(jnp.where(lanes == k, value, 0.0), axis=1, keepdims=True)
        pivot = jnp.sum(jnp.where(lanes[:1] == k, pivot_row, 0.0), axis=1, keepdims=True)
        factor = jnp.where(rows[:, :1] > k, column / pivot, 0.0)
        aug[...] = value - factor * pivot_row
        return carry

    lax.fori_loop(0, rank // 2, eliminate, 0)

    wait_bytes(g_in, g_sem.at[1])
    total = tile(g_own, x, row)[...]
    for k in range(n_dev - 1):
        total = total + g_in[k]
    gz_in[z] = total
    for k in range(1, nz):
        remote(gz_in.at[z], gz_in.at[z], g_sem.at[2], g_sem.at[3], (away(z, k, nz), d)).start()

    lax.fori_loop(rank // 2, rank, eliminate, 0)
    final = aug[...]
    diagonal = jnp.sum(jnp.where(rows == lanes, final, 0.0), axis=1, keepdims=True)
    inverse = final[:, rank:] * (1.0 / jnp.sqrt(diagonal))
    i_high, i_low = halves(inverse)

    wait_bytes(gz_in.at[pl.ds(0, nz - 1)], g_sem.at[3])
    total = gz_in[0]
    for k in range(1, nz):
        total = total + gz_in[k]
    mine = tile(g_full, x, row)
    mine[...] = total
    for k in range(1, n_dev):
        remote(mine, mine, g_sem.at[4], g_sem.at[5], (z, away(d, k, n_dev))).start()

    left = jnp.concatenate([i_high, i_high, i_low], axis=1)

    def applied(value):
        high, low = halves(value)
        return mm(left, jnp.concatenate([high, low, high], axis=0))

    for a in range(pieces):
        value = applied(full[a].reshape(rank, width))
        phat_ref[:, a * width:(a + 1) * width] = value

    wait_bytes(g_in, g_sem.at[5])
    q_mean = applied(g_full[...]) * (1.0 / devices)
    qmean_ref[...] = q_mean
    high, low = halves(q_mean)
    right = jnp.concatenate([high, high, low], axis=0)
    for a in range(pieces):
        high, low = halves(phat_ref[:, a * width:(a + 1) * width])
        value = merged[a] - mm(jnp.concatenate([high, low, high], axis=0), right, 0, 0)
        out_ref[a * width:(a + 1) * width, :] = value.astype(BF16)

    for i in range(pieces):
        core_copy(i).wait_send()
    wait_bytes(plane_in, rs_send)
    wait_bytes(z_in.at[:, pl.ds(0, nz - 1)], z_send)
    wait_bytes(plane_in, ag_send)
    wait_bytes(core_in, fw_send)
    wait_bytes(g_in, g_sem.at[0])
    wait_bytes(gz_in.at[pl.ds(0, nz - 1)], g_sem.at[2])
    wait_bytes(g_in, g_sem.at[4])


def step(nx, ny, nz, inputs, cotangent, errors, previous_q):
    tok, width = inputs.shape
    kvw = cotangent.shape[1]
    rank = previous_q.shape[1]
    subs = SUBS
    pieces = nx * subs
    w = width // pieces
    group = rank // (2 * ny)
    n_dev = 2 * nx * ny
    dma = pltpu.SemaphoreType.DMA
    any_space = pl.BlockSpec(memory_space=pl.ANY)
    vmem = pl.BlockSpec(memory_space=pltpu.VMEM)
    new_errors, p_hat, q_mean = pl.pallas_call(
        functools.partial(kernel, nx, ny, nz),
        out_shape=(
            jax.ShapeDtypeStruct((width, kvw), BF16),
            jax.ShapeDtypeStruct((rank, width), F32),
            jax.ShapeDtypeStruct((rank, kvw), F32),
        ),
        in_specs=[any_space, any_space, any_space, vmem],
        out_specs=(vmem, vmem, vmem),
        scratch_shapes=[
            pltpu.VMEM((pieces, tok, w), BF16),
            pltpu.VMEM((pieces, w, kvw), BF16),
            pltpu.VMEM((tok, kvw), BF16),
            pltpu.VMEM((pieces, w, kvw), F32),
            pltpu.VMEM((pieces, w, kvw), BF16),
            pltpu.VMEM((pieces, w, kvw), BF16),
            pltpu.VMEM((4 * rank, kvw), BF16),
            pltpu.VMEM((pieces, 2 * ny, group, w), F32),
            pltpu.VMEM((pieces, ny, group, w), F32),
            pltpu.VMEM((pieces, ny, group, w), F32),
            pltpu.VMEM((subs, nx * ny - 1, group, w), F32),
            pltpu.VMEM((subs, nz, group, w), F32),
            pltpu.VMEM((pieces, 2 * ny, group, w), F32),
            pltpu.VMEM((rank, kvw), F32),
            pltpu.VMEM((n_dev - 1, group, kvw // nx), F32),
            pltpu.VMEM((nz, group, kvw // nx), F32),
            pltpu.VMEM((group, kvw // nx), F32),
            pltpu.VMEM((rank, kvw), F32),
            pltpu.VMEM((rank, 2 * rank), F32),
            dma((3, pieces)),
            dma((pieces,)),
            dma((pieces,)),
            dma(()),
            dma((subs,)),
            dma(()),
            dma((subs,)),
            dma(()),
            dma((subs, nx)),
            dma(()),
            dma((subs, nx)),
            dma((6,)),
        ],
        compiler_params=pltpu.CompilerParams(
            collective_id=0, has_side_effects=True, vmem_limit_bytes=40 * 2**20
        ),
        name="powersgd",
    )(inputs, cotangent, errors, previous_q.T)
    return new_errors[None], p_hat.T, q_mean.T


def solution(mesh):
    nz = mesh.shape["cuts"]
    side = 1
    while 2 * side * side < mesh.shape["dev"]:
        side *= 2
    in_specs = (
        P(("cuts", "dev"), None),
        P(("cuts", "dev"), None),
        P(("cuts", "dev"), None, None),
        P(),
    )
    out_specs = (P(("cuts", "dev"), None, None), P(), P())
    return jax.shard_map(
        functools.partial(step, side, side, nz), mesh=mesh, in_specs=in_specs, out_specs=out_specs, check_vma=False
    )
```

```python
import functools

import jax
import jax.numpy as jnp
from jax import lax
from jax.experimental import pallas as pl
from jax.experimental.pallas import tpu as pltpu
from jax.sharding import PartitionSpec as P

MESH = pl.DeviceIdType.MESH
F32 = jnp.float32
BF16 = jnp.bfloat16
SUBS = 2


def halves(value):
    high = value.astype(BF16)
    low = (value - high.astype(F32)).astype(BF16)
    return high, low


def mm(left, right, left_dim=1, right_dim=0):
    return lax.dot_general(
        left, right, (((left_dim,), (right_dim,)), ((), ())), preferred_element_type=F32
    )


def far_first(n):
    return sorted(range(n), key=lambda step: -min(step, n - step))


def kernel(
    nx, ny, nz,
    x_hbm, y_hbm, e_hbm, qt_hbm,
    merged, left_parts, phat_ref, qmean_ref,
    xv, ev, yv, qt_ref, m_high, m_low, base,
    part, core_in, chip_sum, plane_in, z_in, full,
    g_own, g_in, gz_in, g_full, aug,
    load_sem, core_send, core_recv, rs_send, rs_recv, z_send, z_recv,
    ag_send, ag_recv, fw_send, fw_recv, g_sem,
):
    subs = SUBS
    rank, kvw = qt_ref.shape
    pieces, tok, width = xv.shape
    group = rank // (2 * ny)
    devices = nx * ny * 2 * nz
    z = lax.axis_index("cuts")
    d = lax.axis_index("dev")
    x, y, c = d // (2 * ny), (d // 2) % ny, d % 2

    def at(xx, yy, cc):
        return (z, (xx * ny + yy) * 2 + cc)

    def away(value, step, n):
        return lax.rem(value + step, n)

    partner = at(x, y, 1 - c)

    def remote(src, dst, send, recv, device):
        return pltpu.make_async_remote_copy(
            src_ref=src, dst_ref=dst, send_sem=send, recv_sem=recv, device_id=device, device_id_type=MESH
        )

    def wait_bytes(ref, sem):
        pltpu.make_async_copy(ref, ref, sem).wait()

    hops = [(dx, dy, dc) for dx in far_first(nx) for dy in far_first(ny) for dc in (0, 1)]
    hops = sorted([h for h in hops if any(h)], key=lambda h: -min(h[0], nx - h[0]) - min(h[1], ny - h[1]))
    plane = [(dx, dy) for dx, dy, dc in hops if dc == 0]

    barrier = pltpu.get_barrier_semaphore()
    for k in far_first(nz):
        if k:
            pl.semaphore_signal(barrier, inc=1, device_id=(away(z, k, nz), d), device_id_type=MESH)
    for dx, dy, dc in hops:
        pl.semaphore_signal(barrier, inc=1, device_id=at(away(x, dx, nx), away(y, dy, ny), away(c, dc, 2)), device_id_type=MESH)

    order = [(s, step) for s in range(subs) for step in far_first(nx)]

    def place(s, step):
        return away(x, step, nx) * subs + s

    q_load = pltpu.make_async_copy(qt_hbm, qt_ref, load_sem.at[2, 1])
    q_load.start()
    y_load = pltpu.make_async_copy(y_hbm, yv, load_sem.at[2, 0])
    y_load.start()
    loads = []
    for i, (s, step) in enumerate(order):
        a = place(s, step)
        start = pl.multiple_of(a * width, width)
        loads.append((
            pltpu.make_async_copy(e_hbm.at[0, pl.ds(start, width), :], ev.at[i], load_sem.at[1, i]),
            pltpu.make_async_copy(x_hbm.at[:, pl.ds(start, width)], xv.at[i], load_sem.at[0, i]),
        ))
        loads[-1][0].start()
        loads[-1][1].start()

    q_load.wait()
    q_high, q_low = halves(qt_ref[...])
    q_two = jnp.concatenate([q_high, q_low], axis=0)
    y_load.wait()
    t_two = mm(q_two, yv[...], 1, 1)
    t_high, t_low = halves(t_two[:rank] + t_two[rank:])
    base[0:rank, :] = t_high
    base[rank:2 * rank, :] = t_low
    base[2 * rank:4 * rank, :] = q_two

    def left_piece(i):
        for load in loads[i]:
            load.wait()
        both = mm(base[0:2 * rank, :], xv[i]) + mm(base[2 * rank:4 * rank, :], ev[i], 1, 1)
        value = both[:rank] + both[rank:]
        part[i] = value.reshape(2 * ny, group, width)

    def core_copy(i):
        return remote(
            part.at[i, pl.ds((1 - c) * ny, ny)], core_in.at[i], core_send.at[i], core_recv.at[i], partner
        )

    def scatter(i):
        s, step = order[i]
        core_copy(i).wait_recv()
        chip_sum[i] = part[i, pl.ds(c * ny, ny)] + core_in[i]
        for dy in far_first(ny):
            if step == 0 and dy == 0:
                continue
            slot = ((nx - step) % nx) * ny + (ny - dy) % ny - 1
            yy = away(y, dy, ny)
            remote(
                chip_sum.at[i, yy], plane_in.at[s, slot], rs_send, rs_recv.at[s], at(away(x, step, nx), yy, c)
            ).start()

    def merge_piece(i):
        s, step = order[i]
        a = place(s, step)
        value = mm(xv[i], yv[...], 0, 0) + ev[i].astype(F32)
        merged[a] = value
        high, low = halves(value)
        m_high[a] = high
        m_low[a] = low

    for i in range(pieces):
        left_piece(i)
    early = pieces // 2
    for i in range(early):
        merge_piece(i)
    pl.semaphore_wait(barrier, len(hops) + nz - 1)
    for i in range(pieces):
        core_copy(i).start()
    for i in range(pieces):
        scatter(i)

    own = [i for i in range(pieces) if order[i][1] == 0]

    def exchange(s):
        wait_bytes(plane_in.at[s], rs_recv.at[s])
        total = chip_sum[own[s], y]
        for slot in range(nx * ny - 1):
            total = total + plane_in[s, slot]
        z_in[s, z] = total
        for k in far_first(nz)[:-1]:
            remote(z_in.at[s, z], z_in.at[s, z], z_send, z_recv.at[s], (away(z, k, nz), d)).start()

    row = c * ny + y

    def spread(s):
        wait_bytes(z_in.at[s, pl.ds(0, nz - 1)], z_recv.at[s])
        total = z_in[s, 0]
        for k in range(1, nz):
            total = total + z_in[s, k]
        a = place(s, 0)
        full[a, row] = total
        for dx, dy in plane:
            remote(
                full.at[a, row], full.at[a, row], ag_send, ag_recv.at[s, (nx - dx) % nx],
                at(away(x, dx, nx), away(y, dy, ny), c),
            ).start()

    rest = list(range(early, pieces))
    for s in range(subs):
        exchange(s)
        for i in rest[s * len(rest) // subs:(s + 1) * len(rest) // subs]:
            merge_piece(i)
    for s in range(subs):
        spread(s)

    arrivals = [(s, rx) for s in range(subs) for rx in reversed(far_first(nx))]

    def forward(s, rx):
        a = place(s, rx)
        count = ny - 1 if rx == 0 else ny
        wait_bytes(full.at[a, pl.ds(c * ny, count)], ag_recv.at[s, rx])
        mine = full.at[a, pl.ds(c * ny, ny)]
        remote(mine, mine, fw_send, fw_recv.at[s, rx], partner).start()

    def right_piece(s, rx, first):
        a = place(s, rx)
        theirs = full.at[a, pl.ds((1 - c) * ny, ny)]
        wait_bytes(theirs, fw_recv.at[s, rx])
        high, low = halves(full[a].reshape(rank, width))
        two = mm(jnp.concatenate([high, low], axis=0), m_high[a])
        value = two[:rank] + two[rank:] + mm(high, m_low[a])
        if first:
            g_own[...] = value
        else:
            g_own[...] += value

    for i, (s, rx) in enumerate(arrivals):
        forward(s, rx)
        if i >= 1:
            right_piece(*arrivals[i - 1], i == 1)
    right_piece(*arrivals[-1], False)

    g_cols = kvw // nx

    def tile(ref, xx, rr):
        return ref.at[pl.ds(pl.multiple_of(rr * group, group), group), pl.ds(pl.multiple_of(xx * g_cols, g_cols), g_cols)]

    for dx, dy, dc in hops:
        tx, ty, tc = away(x, dx, nx), away(y, dy, ny), away(c, dc, 2)
        slot = ((nx - dx) % nx * ny + (ny - dy) % ny) * 2 + dc - 1
        remote(tile(g_own, tx, tc * ny + ty), g_in.at[slot], g_sem.at[0], g_sem.at[1], at(tx, ty, tc)).start()

    gram = jnp.zeros((2 * rank, 2 * rank), F32)
    for a in range(pieces):
        high, low = halves(full[a].reshape(rank, width))
        two = jnp.concatenate([high, low], axis=0)
        gram = gram + mm(two, two, 1, 1)
    gram = gram[:rank] + gram[rank:]
    gram = gram[:, :rank] + gram[:, rank:]
    rows = lax.broadcasted_iota(jnp.int32, (rank, 2 * rank), 0)
    lanes = lax.broadcasted_iota(jnp.int32, (rank, 2 * rank), 1)
    aug[:, 0:rank] = gram
    aug[:, rank:2 * rank] = (rows == lanes).astype(F32)[:, :rank]

    def eliminate(k, carry):
        value = aug[...]
        pivot_row = aug[pl.ds(k, 1), :]
        column = jnp.sum(jnp.where(lanes == k, value, 0.0), axis=1, keepdims=True)
        pivot = jnp.sum(jnp.where(lanes[:1] == k, pivot_row, 0.0), axis=1, keepdims=True)
        factor = jnp.where(rows[:, :1] > k, column / pivot, 0.0)
        aug[...] = value - factor * pivot_row
        return carry

    lax.fori_loop(0, rank // 2, eliminate, 0)

    wait_bytes(g_in, g_sem.at[1])
    total = tile(g_own, x, row)[...]
    for k in range(len(hops)):
        total = total + g_in[k]
    gz_in[z] = total
    for k in far_first(nz)[:-1]:
        remote(gz_in.at[z], gz_in.at[z], g_sem.at[2], g_sem.at[3], (away(z, k, nz), d)).start()

    lax.fori_loop(rank // 2, rank, eliminate, 0)
    final = aug[...]
    diagonal = jnp.sum(jnp.where(rows == lanes, final, 0.0), axis=1, keepdims=True)
    inverse = final[:, rank:] * (1.0 / jnp.sqrt(diagonal))
    i_high, i_low = halves(inverse)

    wait_bytes(gz_in.at[pl.ds(0, nz - 1)], g_sem.at[3])
    total = gz_in[0]
    for k in range(1, nz):
        total = total + gz_in[k]
    mine = tile(g_full, x, row)
    mine[...] = total
    for dx, dy, dc in hops:
        to = at(away(x, dx, nx), away(y, dy, ny), away(c, dc, 2))
        remote(mine, mine, g_sem.at[4], g_sem.at[5], to).start()

    left = jnp.concatenate([i_high, i_high, i_low], axis=1)

    def applied(value):
        high, low = halves(value)
        return mm(left, jnp.concatenate([high, low, high], axis=0))

    for a in range(pieces):
        value = applied(full[a].reshape(rank, width))
        phat_ref[:, a * width:(a + 1) * width] = value
        high, low = halves(value)
        left_parts[a] = jnp.concatenate([high, low, high], axis=0).T

    wait_bytes(g_in, g_sem.at[5])
    q_mean = applied(g_full[...]) * (1.0 / devices)
    qmean_ref[...] = q_mean

    for i in range(pieces):
        core_copy(i).wait_send()
    wait_bytes(plane_in, rs_send)
    wait_bytes(z_in.at[:, pl.ds(0, nz - 1)], z_send)
    wait_bytes(plane_in, ag_send)
    wait_bytes(core_in, fw_send)
    wait_bytes(g_in, g_sem.at[0])
    wait_bytes(gz_in.at[pl.ds(0, nz - 1)], g_sem.at[2])
    wait_bytes(g_in, g_sem.at[4])


def finish(merged, left_parts, phat_ref, qmean_ref, out_hbm, phat_hbm, qmean_hbm, rows, row_sem, small_sem):
    pieces, width, kvw = merged.shape
    small = (
        pltpu.make_async_copy(phat_ref, phat_hbm, small_sem.at[0]),
        pltpu.make_async_copy(qmean_ref, qmean_hbm, small_sem.at[1]),
    )
    for copy in small:
        copy.start()
    high, low = halves(qmean_ref[...])
    right = jnp.concatenate([high, high, low], axis=0)
    copies = []
    for a in range(pieces):
        rows[a] = (merged[a] - mm(left_parts[a], right)).astype(BF16)
        copies.append(pltpu.make_async_copy(rows.at[a], out_hbm.at[pl.ds(a * width, width), :], row_sem.at[a]))
        copies[-1].start()
    for copy in (*small, *copies):
        copy.wait()


def step(nx, ny, nz, inputs, cotangent, errors, previous_q):
    tok, width = inputs.shape
    kvw = cotangent.shape[1]
    rank = previous_q.shape[1]
    subs = SUBS
    pieces = nx * subs
    w = width // pieces
    group = rank // (2 * ny)
    n_dev = 2 * nx * ny
    dma = pltpu.SemaphoreType.DMA
    hbm = pl.BlockSpec(memory_space=pltpu.HBM)
    vmem = pl.BlockSpec(memory_space=pltpu.VMEM)
    merged, left_parts, p_hat, q_mean = pl.pallas_call(
        functools.partial(kernel, nx, ny, nz),
        out_shape=(
            jax.ShapeDtypeStruct((pieces, w, kvw), F32),
            jax.ShapeDtypeStruct((pieces, w, 3 * rank), BF16),
            jax.ShapeDtypeStruct((rank, width), F32),
            jax.ShapeDtypeStruct((rank, kvw), F32),
        ),
        in_specs=[hbm, hbm, hbm, hbm],
        out_specs=(vmem, vmem, vmem, vmem),
        scratch_shapes=[
            pltpu.VMEM((pieces, tok, w), BF16),
            pltpu.VMEM((pieces, w, kvw), BF16),
            pltpu.VMEM((tok, kvw), BF16),
            pltpu.VMEM((rank, kvw), F32),
            pltpu.VMEM((pieces, w, kvw), BF16),
            pltpu.VMEM((pieces, w, kvw), BF16),
            pltpu.VMEM((4 * rank, kvw), BF16),
            pltpu.VMEM((pieces, 2 * ny, group, w), F32),
            pltpu.VMEM((pieces, ny, group, w), F32),
            pltpu.VMEM((pieces, ny, group, w), F32),
            pltpu.VMEM((subs, nx * ny - 1, group, w), F32),
            pltpu.VMEM((subs, nz, group, w), F32),
            pltpu.VMEM((pieces, 2 * ny, group, w), F32),
            pltpu.VMEM((rank, kvw), F32),
            pltpu.VMEM((n_dev - 1, group, kvw // nx), F32),
            pltpu.VMEM((nz, group, kvw // nx), F32),
            pltpu.VMEM((rank, kvw), F32),
            pltpu.VMEM((rank, 2 * rank), F32),
            dma((3, pieces)),
            dma((pieces,)),
            dma((pieces,)),
            dma(()),
            dma((subs,)),
            dma(()),
            dma((subs,)),
            dma(()),
            dma((subs, nx)),
            dma(()),
            dma((subs, nx)),
            dma((6,)),
        ],
        compiler_params=pltpu.CompilerParams(
            collective_id=0, has_side_effects=True, vmem_limit_bytes=36 * 2**20
        ),
        name="powersgd",
    )(*[pltpu.with_memory_space_constraint(a, pltpu.HBM) for a in (inputs, cotangent, errors, previous_q.T)])
    new_errors, p_hat, q_mean = pl.pallas_call(
        finish,
        out_shape=(
            jax.ShapeDtypeStruct((width, kvw), BF16),
            jax.ShapeDtypeStruct((rank, width), F32),
            jax.ShapeDtypeStruct((rank, kvw), F32),
        ),
        in_specs=[vmem, vmem, vmem, vmem],
        out_specs=(hbm, hbm, hbm),
        scratch_shapes=[pltpu.VMEM((pieces, w, kvw), BF16), dma((pieces,)), dma((2,))],
        compiler_params=pltpu.CompilerParams(vmem_limit_bytes=24 * 2**20),
        name="new_errors",
    )(merged, left_parts, p_hat, q_mean)
    return new_errors[None], p_hat.T, q_mean.T


def solution(mesh):
    nz = mesh.shape["cuts"]
    side = 1
    while 2 * side * side < mesh.shape["dev"]:
        side *= 2
    in_specs = (
        P(("cuts", "dev"), None),
        P(("cuts", "dev"), None),
        P(("cuts", "dev"), None, None),
        P(),
    )
    out_specs = (P(("cuts", "dev"), None, None), P(), P())
    return jax.shard_map(
        functools.partial(step, side, side, nz), mesh=mesh, in_specs=in_specs, out_specs=out_specs, check_vma=False
    )
```

```python
import functools

import jax
import jax.numpy as jnp
from jax import lax
from jax.experimental import pallas as pl
from jax.experimental.pallas import tpu as pltpu
from jax.sharding import PartitionSpec as P

MESH = pl.DeviceIdType.MESH
F32 = jnp.float32
BF16 = jnp.bfloat16
SUBS = 2


def halves(value):
    high = value.astype(BF16)
    low = (value - high.astype(F32)).astype(BF16)
    return high, low


def mm(left, right, left_dim=1, right_dim=0):
    return lax.dot_general(
        left, right, (((left_dim,), (right_dim,)), ((), ())), preferred_element_type=F32
    )


def far_first(n):
    return sorted(range(n), key=lambda step: -min(step, n - step))


def kernel(
    nx, ny, nz,
    x_hbm, y_hbm, e_hbm, qt_hbm,
    merged, left_parts, phat_ref, qmean_ref,
    xv, ev, yv, qt_ref, m_high, m_low, base,
    part, core_in, chip_sum, line_in, line_sum, cell_in, z_in, full,
    g_own, g_in, gz_in, g_full, aug,
    load_sem, core_send, core_recv, rs_send, rs_recv, cell_send, cell_recv, z_send, z_recv,
    ag_send, ag_recv, fw_send, fw_recv, g_sem,
):
    subs = SUBS
    rank, kvw = qt_ref.shape
    pieces, tok, width = xv.shape
    group = rank // (2 * ny)
    devices = nx * ny * 2 * nz
    z = lax.axis_index("cuts")
    d = lax.axis_index("dev")
    x, y, c = d // (2 * ny), (d // 2) % ny, d % 2

    def at(xx, yy, cc):
        return (z, (xx * ny + yy) * 2 + cc)

    def away(value, step, n):
        return lax.rem(value + step, n)

    partner = at(x, y, 1 - c)

    def remote(src, dst, send, recv, device):
        return pltpu.make_async_remote_copy(
            src_ref=src, dst_ref=dst, send_sem=send, recv_sem=recv, device_id=device, device_id_type=MESH
        )

    def wait_bytes(ref, sem):
        pltpu.make_async_copy(ref, ref, sem).wait()

    hops = [(dx, dy, dc) for dx in far_first(nx) for dy in far_first(ny) for dc in (0, 1)]
    hops = sorted([h for h in hops if any(h)], key=lambda h: -min(h[0], nx - h[0]) - min(h[1], ny - h[1]))
    plane = [(dx, dy) for dx, dy, dc in hops if dc == 0]

    barrier = pltpu.get_barrier_semaphore()
    for k in far_first(nz):
        if k:
            pl.semaphore_signal(barrier, inc=1, device_id=(away(z, k, nz), d), device_id_type=MESH)
    for dx, dy, dc in hops:
        pl.semaphore_signal(barrier, inc=1, device_id=at(away(x, dx, nx), away(y, dy, ny), away(c, dc, 2)), device_id_type=MESH)

    order = [(s, step) for s in range(subs) for step in far_first(nx)]

    def place(s, step):
        return away(x, step, nx) * subs + s

    q_load = pltpu.make_async_copy(qt_hbm, qt_ref, load_sem.at[2, 1])
    q_load.start()
    y_load = pltpu.make_async_copy(y_hbm, yv, load_sem.at[2, 0])
    y_load.start()
    loads = []
    for i, (s, step) in enumerate(order):
        a = place(s, step)
        start = pl.multiple_of(a * width, width)
        loads.append((
            pltpu.make_async_copy(e_hbm.at[0, pl.ds(start, width), :], ev.at[i], load_sem.at[1, i]),
            pltpu.make_async_copy(x_hbm.at[:, pl.ds(start, width)], xv.at[i], load_sem.at[0, i]),
        ))
        loads[-1][0].start()
        loads[-1][1].start()

    q_load.wait()
    q_high, q_low = halves(qt_ref[...])
    q_two = jnp.concatenate([q_high, q_low], axis=0)
    y_load.wait()
    t_two = mm(q_two, yv[...], 1, 1)
    t_high, t_low = halves(t_two[:rank] + t_two[rank:])
    base[0:rank, :] = t_high
    base[rank:2 * rank, :] = t_low
    base[2 * rank:4 * rank, :] = q_two

    def left_piece(i):
        for load in loads[i]:
            load.wait()
        both = mm(base[0:2 * rank, :], xv[i]) + mm(base[2 * rank:4 * rank, :], ev[i], 1, 1)
        value = both[:rank] + both[rank:]
        part[i] = value.reshape(2 * ny, group, width)

    def core_copy(i):
        return remote(
            part.at[i, pl.ds((1 - c) * ny, ny)], core_in.at[i], core_send.at[i], core_recv.at[i], partner
        )

    def scatter(i):
        s, step = order[i]
        core_copy(i).wait_recv()
        chip_sum[i] = part[i, pl.ds(c * ny, ny)] + core_in[i]
        if step:
            @pl.when(c == 0)
            def _():
                slot = (nx - step) % nx - 1
                to = at(away(x, step, nx), y, c)
                remote(chip_sum.at[i], line_in.at[s, slot], rs_send, rs_recv.at[s], to).start()
        else:
            @pl.when(c == 1)
            def _():
                for dy in far_first(ny)[:-1]:
                    yy = away(y, dy, ny)
                    remote(
                        chip_sum.at[pl.ds(s * nx, nx), yy], line_in.at[s, (ny - dy) % ny - 1],
                        rs_send, rs_recv.at[s], at(x, yy, c),
                    ).start()

    def merge_piece(i):
        s, step = order[i]
        a = place(s, step)
        value = mm(xv[i], yv[...], 0, 0) + ev[i].astype(F32)
        merged[a] = value
        high, low = halves(value)
        m_high[a] = high
        m_low[a] = low

    for i in range(pieces):
        left_piece(i)
    early = pieces // 2
    for i in range(early):
        merge_piece(i)
    pl.semaphore_wait(barrier, len(hops) + nz - 1)
    for i in range(pieces):
        core_copy(i).start()
    for i in range(pieces):
        scatter(i)

    own = [i for i in range(pieces) if order[i][1] == 0]

    def line(s):
        wait_bytes(line_in.at[s], rs_recv.at[s])
        total = line_in[s, 0]
        for k in range(1, nx - 1):
            total = total + line_in[s, k]

        @pl.when(c == 0)
        def _():
            line_sum[s] = total + chip_sum[own[s]]
            for dy in far_first(ny)[:-1]:
                yy = away(y, dy, ny)
                remote(
                    line_sum.at[s, yy], cell_in.at[s, (ny - dy) % ny - 1], cell_send, cell_recv.at[s], at(x, yy, c)
                ).start()

        @pl.when(c == 1)
        def _():
            line_sum[s] = total + chip_sum[pl.ds(s * nx, nx), y]
            for t, step in enumerate(far_first(nx)[:-1]):
                to = at(away(x, step, nx), y, c)
                remote(
                    line_sum.at[s, t], cell_in.at[s, (nx - step) % nx - 1], cell_send, cell_recv.at[s], to
                ).start()

    def exchange(s):
        wait_bytes(cell_in.at[s], cell_recv.at[s])
        total = line_sum[s, (1 - c) * y + c * (nx - 1)]
        for k in range(nx - 1):
            total = total + cell_in[s, k]
        z_in[s, z] = total
        for k in far_first(nz)[:-1]:
            remote(z_in.at[s, z], z_in.at[s, z], z_send, z_recv.at[s], (away(z, k, nz), d)).start()

    row = c * ny + y

    def spread(s):
        wait_bytes(z_in.at[s, pl.ds(0, nz - 1)], z_recv.at[s])
        total = z_in[s, 0]
        for k in range(1, nz):
            total = total + z_in[s, k]
        a = place(s, 0)
        full[a, row] = total
        for dx, dy in plane:
            remote(
                full.at[a, row], full.at[a, row], ag_send, ag_recv.at[s, (nx - dx) % nx],
                at(away(x, dx, nx), away(y, dy, ny), c),
            ).start()

    for s in range(subs):
        line(s)
    rest = list(range(early, pieces))
    for s in range(subs):
        exchange(s)
        for i in rest[s * len(rest) // subs:(s + 1) * len(rest) // subs]:
            merge_piece(i)
    for s in range(subs):
        spread(s)

    arrivals = [(s, rx) for s in range(subs) for rx in reversed(far_first(nx))]

    def forward(s, rx):
        a = place(s, rx)
        count = ny - 1 if rx == 0 else ny
        wait_bytes(full.at[a, pl.ds(c * ny, count)], ag_recv.at[s, rx])
        mine = full.at[a, pl.ds(c * ny, ny)]
        remote(mine, mine, fw_send, fw_recv.at[s, rx], partner).start()

    def right_piece(s, rx, first):
        a = place(s, rx)
        theirs = full.at[a, pl.ds((1 - c) * ny, ny)]
        wait_bytes(theirs, fw_recv.at[s, rx])
        high, low = halves(full[a].reshape(rank, width))
        two = mm(jnp.concatenate([high, low], axis=0), m_high[a])
        value = two[:rank] + two[rank:] + mm(high, m_low[a])
        if first:
            g_own[...] = value
        else:
            g_own[...] += value

    for i, (s, rx) in enumerate(arrivals):
        forward(s, rx)
        if i >= 1:
            right_piece(*arrivals[i - 1], i == 1)
    right_piece(*arrivals[-1], False)

    g_cols = kvw // nx

    def tile(ref, xx, rr):
        return ref.at[pl.ds(pl.multiple_of(rr * group, group), group), pl.ds(pl.multiple_of(xx * g_cols, g_cols), g_cols)]

    for dx, dy, dc in hops:
        tx, ty, tc = away(x, dx, nx), away(y, dy, ny), away(c, dc, 2)
        slot = ((nx - dx) % nx * ny + (ny - dy) % ny) * 2 + dc - 1
        remote(tile(g_own, tx, tc * ny + ty), g_in.at[slot], g_sem.at[0], g_sem.at[1], at(tx, ty, tc)).start()

    gram = jnp.zeros((2 * rank, 2 * rank), F32)
    for a in range(pieces):
        high, low = halves(full[a].reshape(rank, width))
        two = jnp.concatenate([high, low], axis=0)
        gram = gram + mm(two, two, 1, 1)
    gram = gram[:rank] + gram[rank:]
    gram = gram[:, :rank] + gram[:, rank:]
    rows = lax.broadcasted_iota(jnp.int32, (rank, 2 * rank), 0)
    lanes = lax.broadcasted_iota(jnp.int32, (rank, 2 * rank), 1)
    aug[:, 0:rank] = gram
    aug[:, rank:2 * rank] = (rows == lanes).astype(F32)[:, :rank]

    def eliminate(k, carry):
        value = aug[...]
        pivot_row = aug[pl.ds(k, 1), :]
        column = jnp.sum(jnp.where(lanes == k, value, 0.0), axis=1, keepdims=True)
        pivot = jnp.sum(jnp.where(lanes[:1] == k, pivot_row, 0.0), axis=1, keepdims=True)
        factor = jnp.where(rows[:, :1] > k, column / pivot, 0.0)
        aug[...] = value - factor * pivot_row
        return carry

    lax.fori_loop(0, rank // 2, eliminate, 0)

    wait_bytes(g_in, g_sem.at[1])
    total = tile(g_own, x, row)[...]
    for k in range(len(hops)):
        total = total + g_in[k]
    gz_in[z] = total
    for k in far_first(nz)[:-1]:
        remote(gz_in.at[z], gz_in.at[z], g_sem.at[2], g_sem.at[3], (away(z, k, nz), d)).start()

    lax.fori_loop(rank // 2, rank, eliminate, 0)
    final = aug[...]
    diagonal = jnp.sum(jnp.where(rows == lanes, final, 0.0), axis=1, keepdims=True)
    inverse = final[:, rank:] * (1.0 / jnp.sqrt(diagonal))
    i_high, i_low = halves(inverse)

    wait_bytes(gz_in.at[pl.ds(0, nz - 1)], g_sem.at[3])
    total = gz_in[0]
    for k in range(1, nz):
        total = total + gz_in[k]
    mine = tile(g_full, x, row)
    mine[...] = total
    for dx, dy, dc in hops:
        to = at(away(x, dx, nx), away(y, dy, ny), away(c, dc, 2))
        remote(mine, mine, g_sem.at[4], g_sem.at[5], to).start()

    left = jnp.concatenate([i_high, i_high, i_low], axis=1)

    def applied(value):
        high, low = halves(value)
        return mm(left, jnp.concatenate([high, low, high], axis=0))

    for a in range(pieces):
        value = applied(full[a].reshape(rank, width))
        phat_ref[:, a * width:(a + 1) * width] = value
        high, low = halves(value)
        left_parts[a] = jnp.concatenate([high, low, high], axis=0).T

    wait_bytes(g_in, g_sem.at[5])
    q_mean = applied(g_full[...]) * (1.0 / devices)
    qmean_ref[...] = q_mean

    for i in range(pieces):
        core_copy(i).wait_send()
    wait_bytes(line_in, rs_send)
    wait_bytes(cell_in, cell_send)
    wait_bytes(z_in.at[:, pl.ds(0, nz - 1)], z_send)
    wait_bytes(part.at[pl.ds(0, 5), pl.ds(0, 6)], ag_send)
    wait_bytes(core_in, fw_send)
    wait_bytes(g_in, g_sem.at[0])
    wait_bytes(gz_in.at[pl.ds(0, nz - 1)], g_sem.at[2])
    wait_bytes(g_in, g_sem.at[4])


def finish(merged, left_parts, phat_ref, qmean_ref, out_hbm, phat_hbm, qmean_hbm, rows, row_sem, small_sem):
    pieces, width, kvw = merged.shape
    small = (
        pltpu.make_async_copy(phat_ref, phat_hbm, small_sem.at[0]),
        pltpu.make_async_copy(qmean_ref, qmean_hbm, small_sem.at[1]),
    )
    for copy in small:
        copy.start()
    high, low = halves(qmean_ref[...])
    right = jnp.concatenate([high, high, low], axis=0)
    copies = []
    for a in range(pieces):
        rows[a] = (merged[a] - mm(left_parts[a], right)).astype(BF16)
        copies.append(pltpu.make_async_copy(rows.at[a], out_hbm.at[pl.ds(a * width, width), :], row_sem.at[a]))
        copies[-1].start()
    for copy in (*small, *copies):
        copy.wait()


def step(nx, ny, nz, inputs, cotangent, errors, previous_q):
    tok, width = inputs.shape
    kvw = cotangent.shape[1]
    rank = previous_q.shape[1]
    subs = SUBS
    pieces = nx * subs
    w = width // pieces
    group = rank // (2 * ny)
    n_dev = 2 * nx * ny
    dma = pltpu.SemaphoreType.DMA
    hbm = pl.BlockSpec(memory_space=pltpu.HBM)
    vmem = pl.BlockSpec(memory_space=pltpu.VMEM)
    merged, left_parts, p_hat, q_mean = pl.pallas_call(
        functools.partial(kernel, nx, ny, nz),
        out_shape=(
            jax.ShapeDtypeStruct((pieces, w, kvw), F32),
            jax.ShapeDtypeStruct((pieces, w, 3 * rank), BF16),
            jax.ShapeDtypeStruct((rank, width), F32),
            jax.ShapeDtypeStruct((rank, kvw), F32),
        ),
        in_specs=[hbm, hbm, hbm, hbm],
        out_specs=(vmem, vmem, vmem, vmem),
        scratch_shapes=[
            pltpu.VMEM((pieces, tok, w), BF16),
            pltpu.VMEM((pieces, w, kvw), BF16),
            pltpu.VMEM((tok, kvw), BF16),
            pltpu.VMEM((rank, kvw), F32),
            pltpu.VMEM((pieces, w, kvw), BF16),
            pltpu.VMEM((pieces, w, kvw), BF16),
            pltpu.VMEM((4 * rank, kvw), BF16),
            pltpu.VMEM((pieces, 2 * ny, group, w), F32),
            pltpu.VMEM((pieces, ny, group, w), F32),
            pltpu.VMEM((pieces, ny, group, w), F32),
            pltpu.VMEM((subs, nx - 1, ny, group, w), F32),
            pltpu.VMEM((subs, ny, group, w), F32),
            pltpu.VMEM((subs, nx - 1, group, w), F32),
            pltpu.VMEM((subs, nz, group, w), F32),
            pltpu.VMEM((pieces, 2 * ny, group, w), F32),
            pltpu.VMEM((rank, kvw), F32),
            pltpu.VMEM((n_dev - 1, group, kvw // nx), F32),
            pltpu.VMEM((nz, group, kvw // nx), F32),
            pltpu.VMEM((rank, kvw), F32),
            pltpu.VMEM((rank, 2 * rank), F32),
            dma((3, pieces)),
            dma((pieces,)),
            dma((pieces,)),
            dma(()),
            dma((subs,)),
            dma(()),
            dma((subs,)),
            dma(()),
            dma((subs,)),
            dma(()),
            dma((subs, nx)),
            dma(()),
            dma((subs, nx)),
            dma((6,)),
        ],
        compiler_params=pltpu.CompilerParams(
            collective_id=0, has_side_effects=True, vmem_limit_bytes=36 * 2**20
        ),
        name="powersgd",
    )(*[pltpu.with_memory_space_constraint(a, pltpu.HBM) for a in (inputs, cotangent, errors, previous_q.T)])
    new_errors, p_hat, q_mean = pl.pallas_call(
        finish,
        out_shape=(
            jax.ShapeDtypeStruct((width, kvw), BF16),
            jax.ShapeDtypeStruct((rank, width), F32),
            jax.ShapeDtypeStruct((rank, kvw), F32),
        ),
        in_specs=[vmem, vmem, vmem, vmem],
        out_specs=(hbm, hbm, hbm),
        scratch_shapes=[pltpu.VMEM((pieces, w, kvw), BF16), dma((pieces,)), dma((2,))],
        compiler_params=pltpu.CompilerParams(vmem_limit_bytes=24 * 2**20),
        name="new_errors",
    )(merged, left_parts, p_hat, q_mean)
    return new_errors[None], p_hat.T, q_mean.T


def solution(mesh):
    nz = mesh.shape["cuts"]
    side = 1
    while 2 * side * side < mesh.shape["dev"]:
        side *= 2
    in_specs = (
        P(("cuts", "dev"), None),
        P(("cuts", "dev"), None),
        P(("cuts", "dev"), None, None),
        P(),
    )
    out_specs = (P(("cuts", "dev"), None, None), P(), P())
    return jax.shard_map(
        functools.partial(step, side, side, nz), mesh=mesh, in_specs=in_specs, out_specs=out_specs, check_vma=False
    )
```

```python
import functools

import jax
import jax.numpy as jnp
from jax import lax
from jax.experimental import pallas as pl
from jax.experimental.pallas import tpu as pltpu
from jax.sharding import PartitionSpec as P

MESH = pl.DeviceIdType.MESH
F32 = jnp.float32
BF16 = jnp.bfloat16
SUBS = 2


def halves(value):
    high = value.astype(BF16)
    low = (value - high.astype(F32)).astype(BF16)
    return high, low


def mm(left, right, left_dim=1, right_dim=0):
    return lax.dot_general(
        left, right, (((left_dim,), (right_dim,)), ((), ())), preferred_element_type=F32
    )


def far_first(n):
    return sorted(range(n), key=lambda step: -min(step, n - step))


def kernel(
    nx, ny, nz,
    x_hbm, y_hbm, e_hbm, qt_hbm,
    merged, left_parts, phat_ref, qmean_ref,
    xv, ev, yv, qt_ref, m_high, m_low, base,
    part, core_in, chip_sum, plane_in, z_in, full,
    g_own, g_in, gz_in, g_full, aug,
    load_sem, core_send, core_recv, rs_send, rs_recv, z_send, z_recv,
    ag_send, ag_recv, fw_send, fw_recv, g_sem,
):
    subs = SUBS
    rank, kvw = qt_ref.shape
    pieces, tok, width = xv.shape
    group = rank // (2 * ny)
    devices = nx * ny * 2 * nz
    z = lax.axis_index("cuts")
    d = lax.axis_index("dev")
    x, y, c = d // (2 * ny), (d // 2) % ny, d % 2

    def at(xx, yy, cc):
        return (z, (xx * ny + yy) * 2 + cc)

    def away(value, step, n):
        return lax.rem(value + step, n)

    partner = at(x, y, 1 - c)

    def remote(src, dst, send, recv, device):
        return pltpu.make_async_remote_copy(
            src_ref=src, dst_ref=dst, send_sem=send, recv_sem=recv, device_id=device, device_id_type=MESH
        )

    def wait_bytes(ref, sem):
        pltpu.make_async_copy(ref, ref, sem).wait()

    hops = [(dx, dy, dc) for dx in far_first(nx) for dy in far_first(ny) for dc in (0, 1)]
    hops = sorted([h for h in hops if any(h)], key=lambda h: -min(h[0], nx - h[0]) - min(h[1], ny - h[1]))
    plane = [(dx, dy) for dx, dy, dc in hops if dc == 0]

    barrier = pltpu.get_barrier_semaphore()
    for k in far_first(nz):
        if k:
            pl.semaphore_signal(barrier, inc=1, device_id=(away(z, k, nz), d), device_id_type=MESH)
    for dx, dy, dc in hops:
        pl.semaphore_signal(barrier, inc=1, device_id=at(away(x, dx, nx), away(y, dy, ny), away(c, dc, 2)), device_id_type=MESH)

    order = [(s, step) for s in range(subs) for step in far_first(nx)]

    def place(s, step):
        return away(x, step, nx) * subs + s

    q_load = pltpu.make_async_copy(qt_hbm, qt_ref, load_sem.at[2, 1])
    q_load.start()
    y_load = pltpu.make_async_copy(y_hbm, yv, load_sem.at[2, 0])
    y_load.start()
    loads = []
    for i, (s, step) in enumerate(order):
        a = place(s, step)
        start = pl.multiple_of(a * width, width)
        loads.append((
            pltpu.make_async_copy(e_hbm.at[0, pl.ds(start, width), :], ev.at[i], load_sem.at[1, i]),
            pltpu.make_async_copy(x_hbm.at[:, pl.ds(start, width)], xv.at[i], load_sem.at[0, i]),
        ))
        loads[-1][0].start()
        loads[-1][1].start()

    q_load.wait()
    q_high, q_low = halves(qt_ref[...])
    q_two = jnp.concatenate([q_high, q_low], axis=0)
    y_load.wait()
    t_two = mm(q_two, yv[...], 1, 1)
    t_high, t_low = halves(t_two[:rank] + t_two[rank:])
    base[0:rank, :] = t_high
    base[rank:2 * rank, :] = t_low
    base[2 * rank:4 * rank, :] = q_two

    def left_piece(i):
        for load in loads[i]:
            load.wait()
        both = mm(base[0:2 * rank, :], xv[i]) + mm(base[2 * rank:4 * rank, :], ev[i], 1, 1)
        value = both[:rank] + both[rank:]
        part[i] = value.reshape(2 * ny, group, width)

    def core_copy(i):
        return remote(
            part.at[i, pl.ds((1 - c) * ny, ny)], core_in.at[i], core_send.at[i], core_recv.at[i], partner
        )

    def scatter(i):
        s, step = order[i]
        core_copy(i).wait_recv()
        chip_sum[i] = part[i, pl.ds(c * ny, ny)] + core_in[i]
        for dy in far_first(ny):
            if step == 0 and dy == 0:
                continue
            slot = ((nx - step) % nx) * ny + (ny - dy) % ny - 1
            yy = away(y, dy, ny)
            remote(
                chip_sum.at[i, yy], plane_in.at[s, slot], rs_send, rs_recv.at[s], at(away(x, step, nx), yy, c)
            ).start()

    def merge_piece(i):
        s, step = order[i]
        a = place(s, step)
        value = mm(xv[i], yv[...], 0, 0) + ev[i].astype(F32)
        merged[a] = value
        high, low = halves(value)
        m_high[a] = high
        m_low[a] = low

    for i in range(pieces):
        left_piece(i)
    early = pieces // 2
    for i in range(early):
        merge_piece(i)
    pl.semaphore_wait(barrier, len(hops) + nz - 1)
    for i in range(pieces):
        core_copy(i).start()
    for i in range(pieces):
        scatter(i)

    own = [i for i in range(pieces) if order[i][1] == 0]

    def exchange(s):
        wait_bytes(plane_in.at[s], rs_recv.at[s])
        total = chip_sum[own[s], y]
        for slot in range(nx * ny - 1):
            total = total + plane_in[s, slot]
        z_in[s, z] = total
        for k in far_first(nz)[:-1]:
            remote(z_in.at[s, z], z_in.at[s, z], z_send, z_recv.at[s], (away(z, k, nz), d)).start()

    row = c * ny + y

    def spread(s):
        wait_bytes(z_in.at[s, pl.ds(0, nz - 1)], z_recv.at[s])
        total = z_in[s, 0]
        for k in range(1, nz):
            total = total + z_in[s, k]
        a = place(s, 0)
        full[a, row] = total
        for dx, dy in plane:
            remote(
                full.at[a, row], full.at[a, row], ag_send, ag_recv.at[s, (nx - dx) % nx],
                at(away(x, dx, nx), away(y, dy, ny), c),
            ).start()

    for i in range(early, pieces):
        merge_piece(i)
    for s in range(subs):
        exchange(s)
    for s in range(subs):
        spread(s)

    arrivals = [(s, rx) for s in range(subs) for rx in reversed(far_first(nx))]

    def forward(s, rx):
        a = place(s, rx)
        count = ny - 1 if rx == 0 else ny
        wait_bytes(full.at[a, pl.ds(c * ny, count)], ag_recv.at[s, rx])
        mine = full.at[a, pl.ds(c * ny, ny)]
        remote(mine, mine, fw_send, fw_recv.at[s, rx], partner).start()

    def right_piece(s, rx, first):
        a = place(s, rx)
        theirs = full.at[a, pl.ds((1 - c) * ny, ny)]
        wait_bytes(theirs, fw_recv.at[s, rx])
        high, low = halves(full[a].reshape(rank, width))
        two = mm(jnp.concatenate([high, low], axis=0), m_high[a])
        value = two[:rank] + two[rank:] + mm(high, m_low[a])
        if first:
            g_own[...] = value
        else:
            g_own[...] += value

    for i, (s, rx) in enumerate(arrivals):
        forward(s, rx)
        if i >= 1:
            right_piece(*arrivals[i - 1], i == 1)
    right_piece(*arrivals[-1], False)

    g_cols = kvw // nx

    def tile(ref, xx, rr):
        return ref.at[pl.ds(pl.multiple_of(rr * group, group), group), pl.ds(pl.multiple_of(xx * g_cols, g_cols), g_cols)]

    for dx, dy, dc in hops:
        tx, ty, tc = away(x, dx, nx), away(y, dy, ny), away(c, dc, 2)
        slot = ((nx - dx) % nx * ny + (ny - dy) % ny) * 2 + dc - 1
        remote(tile(g_own, tx, tc * ny + ty), g_in.at[slot], g_sem.at[0], g_sem.at[1], at(tx, ty, tc)).start()

    gram = jnp.zeros((2 * rank, 2 * rank), F32)
    for a in range(pieces):
        high, low = halves(full[a].reshape(rank, width))
        two = jnp.concatenate([high, low], axis=0)
        gram = gram + mm(two, two, 1, 1)
    gram = gram[:rank] + gram[rank:]
    gram = gram[:, :rank] + gram[:, rank:]
    rows = lax.broadcasted_iota(jnp.int32, (rank, 2 * rank), 0)
    lanes = lax.broadcasted_iota(jnp.int32, (rank, 2 * rank), 1)
    aug[:, 0:rank] = gram
    aug[:, rank:2 * rank] = (rows == lanes).astype(F32)[:, :rank]

    def eliminate(k, carry):
        value = aug[...]
        pivot_row = aug[pl.ds(k, 1), :]
        column = jnp.sum(jnp.where(lanes == k, value, 0.0), axis=1, keepdims=True)
        pivot = jnp.sum(jnp.where(lanes[:1] == k, pivot_row, 0.0), axis=1, keepdims=True)
        factor = jnp.where(rows[:, :1] > k, column / pivot, 0.0)
        aug[...] = value - factor * pivot_row
        return carry

    lax.fori_loop(0, rank // 2, eliminate, 0)

    wait_bytes(g_in, g_sem.at[1])
    total = tile(g_own, x, row)[...]
    for k in range(len(hops)):
        total = total + g_in[k]
    gz_in[z] = total
    for k in far_first(nz)[:-1]:
        remote(gz_in.at[z], gz_in.at[z], g_sem.at[2], g_sem.at[3], (away(z, k, nz), d)).start()

    lax.fori_loop(rank // 2, rank, eliminate, 0)
    final = aug[...]
    diagonal = jnp.sum(jnp.where(rows == lanes, final, 0.0), axis=1, keepdims=True)
    inverse = final[:, rank:] * (1.0 / jnp.sqrt(diagonal))
    i_high, i_low = halves(inverse)

    wait_bytes(gz_in.at[pl.ds(0, nz - 1)], g_sem.at[3])
    total = gz_in[0]
    for k in range(1, nz):
        total = total + gz_in[k]
    mine = tile(g_full, x, row)
    mine[...] = total
    for dx, dy, dc in hops:
        to = at(away(x, dx, nx), away(y, dy, ny), away(c, dc, 2))
        remote(mine, mine, g_sem.at[4], g_sem.at[5], to).start()

    left = jnp.concatenate([i_high, i_high, i_low], axis=1)

    def applied(value):
        high, low = halves(value)
        return mm(left, jnp.concatenate([high, low, high], axis=0))

    for a in range(pieces):
        value = applied(full[a].reshape(rank, width))
        phat_ref[:, a * width:(a + 1) * width] = value
        high, low = halves(value)
        left_parts[a] = jnp.concatenate([high, low, high], axis=0).T

    wait_bytes(g_in, g_sem.at[5])
    q_mean = applied(g_full[...]) * (1.0 / devices)
    qmean_ref[...] = q_mean

    for i in range(pieces):
        core_copy(i).wait_send()
    wait_bytes(plane_in, rs_send)
    wait_bytes(z_in.at[:, pl.ds(0, nz - 1)], z_send)
    wait_bytes(plane_in, ag_send)
    wait_bytes(core_in, fw_send)
    wait_bytes(g_in, g_sem.at[0])
    wait_bytes(gz_in.at[pl.ds(0, nz - 1)], g_sem.at[2])
    wait_bytes(g_in, g_sem.at[4])


def finish(merged, left_parts, phat_ref, qmean_ref, out_hbm, phat_hbm, qmean_hbm, rows, row_sem, small_sem):
    pieces, width, kvw = merged.shape
    small = (
        pltpu.make_async_copy(phat_ref, phat_hbm, small_sem.at[0]),
        pltpu.make_async_copy(qmean_ref, qmean_hbm, small_sem.at[1]),
    )
    for copy in small:
        copy.start()
    high, low = halves(qmean_ref[...])
    right = jnp.concatenate([high, high, low], axis=0)
    copies = []
    for a in range(pieces):
        rows[a] = (merged[a] - mm(left_parts[a], right)).astype(BF16)
        copies.append(pltpu.make_async_copy(rows.at[a], out_hbm.at[pl.ds(a * width, width), :], row_sem.at[a]))
        copies[-1].start()
    for copy in (*small, *copies):
        copy.wait()


def step(nx, ny, nz, inputs, cotangent, errors, previous_q):
    tok, width = inputs.shape
    kvw = cotangent.shape[1]
    rank = previous_q.shape[1]
    subs = SUBS
    pieces = nx * subs
    w = width // pieces
    group = rank // (2 * ny)
    n_dev = 2 * nx * ny
    dma = pltpu.SemaphoreType.DMA
    hbm = pl.BlockSpec(memory_space=pltpu.HBM)
    vmem = pl.BlockSpec(memory_space=pltpu.VMEM)
    merged, left_parts, p_hat, q_mean = pl.pallas_call(
        functools.partial(kernel, nx, ny, nz),
        out_shape=(
            jax.ShapeDtypeStruct((pieces, w, kvw), F32),
            jax.ShapeDtypeStruct((pieces, w, 3 * rank), BF16),
            jax.ShapeDtypeStruct((rank, width), F32),
            jax.ShapeDtypeStruct((rank, kvw), F32),
        ),
        in_specs=[hbm, hbm, hbm, hbm],
        out_specs=(vmem, vmem, vmem, vmem),
        scratch_shapes=[
            pltpu.VMEM((pieces, tok, w), BF16),
            pltpu.VMEM((pieces, w, kvw), BF16),
            pltpu.VMEM((tok, kvw), BF16),
            pltpu.VMEM((rank, kvw), F32),
            pltpu.VMEM((pieces, w, kvw), BF16),
            pltpu.VMEM((pieces, w, kvw), BF16),
            pltpu.VMEM((4 * rank, kvw), BF16),
            pltpu.VMEM((pieces, 2 * ny, group, w), F32),
            pltpu.VMEM((pieces, ny, group, w), F32),
            pltpu.VMEM((pieces, ny, group, w), F32),
            pltpu.VMEM((subs, nx * ny - 1, group, w), F32),
            pltpu.VMEM((subs, nz, group, w), F32),
            pltpu.VMEM((pieces, 2 * ny, group, w), F32),
            pltpu.VMEM((rank, kvw), F32),
            pltpu.VMEM((n_dev - 1, group, kvw // nx), F32),
            pltpu.VMEM((nz, group, kvw // nx), F32),
            pltpu.VMEM((rank, kvw), F32),
            pltpu.VMEM((rank, 2 * rank), F32),
            dma((3, pieces)),
            dma((pieces,)),
            dma((pieces,)),
            dma(()),
            dma((subs,)),
            dma(()),
            dma((subs,)),
            dma(()),
            dma((subs, nx)),
            dma(()),
            dma((subs, nx)),
            dma((6,)),
        ],
        compiler_params=pltpu.CompilerParams(
            collective_id=0, has_side_effects=True, vmem_limit_bytes=36 * 2**20
        ),
        name="powersgd",
    )(*[pltpu.with_memory_space_constraint(a, pltpu.HBM) for a in (inputs, cotangent, errors, previous_q.T)])
    new_errors, p_hat, q_mean = pl.pallas_call(
        finish,
        out_shape=(
            jax.ShapeDtypeStruct((width, kvw), BF16),
            jax.ShapeDtypeStruct((rank, width), F32),
            jax.ShapeDtypeStruct((rank, kvw), F32),
        ),
        in_specs=[vmem, vmem, vmem, vmem],
        out_specs=(hbm, hbm, hbm),
        scratch_shapes=[pltpu.VMEM((pieces, w, kvw), BF16), dma((pieces,)), dma((2,))],
        compiler_params=pltpu.CompilerParams(vmem_limit_bytes=24 * 2**20),
        name="new_errors",
    )(merged, left_parts, p_hat, q_mean)
    return new_errors[None], p_hat.T, q_mean.T


def solution(mesh):
    nz = mesh.shape["cuts"]
    side = 1
    while 2 * side * side < mesh.shape["dev"]:
        side *= 2
    in_specs = (
        P(("cuts", "dev"), None),
        P(("cuts", "dev"), None),
        P(("cuts", "dev"), None, None),
        P(),
    )
    out_specs = (P(("cuts", "dev"), None, None), P(), P())
    return jax.shard_map(
        functools.partial(step, side, side, nz), mesh=mesh, in_specs=in_specs, out_specs=out_specs, check_vma=False
    )
```
